32 devices in a mesh: shard: 8 (over y, x, core), rep: 4 (over z).
Axes of the slice: x: 2, y: 2, z: 4, core: 2. Of those that a mesh axis runs over, the one named last changes fastest.
Arguments:
- grad_parts: bfloat16 [4, 512, 8192], P('rep', 'shard'), may hold values from -12 to 12
- owner_plan: int32 [4, 4], P('rep'), may hold values from 0 to 7, as said below
- refresh: int32 [4, 2], P('rep'), may hold values from 0 to 7, as said below
- roots: bfloat16 [4, 8, 2, 512, 512], P('rep', 'shard'), may hold values from -0.02 to 0.52
Outputs:
- update: bfloat16 [512, 8192], P('shard', 'rep')
The draws below stay inside these ranges and needn't reach their ends.
Inputs may be any that keep to these rules, and one draw needn't show every extreme that they name: `owner_plan`: within each replica's row the 4 owners are distinct; otherwise the assignment is arbitrary. `refresh`: entry 2 b + s names side s (0 left, 1 right) of block b of the row's replica; no block appears twice in a row.
All inputs are finite; a program needn't handle non-finite values.
Results may differ from the reference program's by a relative error of at most 0.018.
Values may be sent and summed in bfloat16 or wider, within the bound.
A program may use at most 64 MiB of HBM per device.

```python
import math
import jax
import jax.numpy as jnp
from jax import lax

BS = 512
NEWTON = 2
BPR = 4
REFRESH = 2
COLS = 8192
N_SHARD = 8
N_REP = 4


def draw_grad_parts(key, part):
    key_list = jax.random.split(jax.random.fold_in(key, 11), 3)
    log_low = math.log(0.3)
    log_high = math.log(3.0)
    row_scale = jnp.exp(jax.random.uniform(key_list[1], (1, BS, 1), jnp.float32, log_low, log_high))
    col_scale = jnp.exp(jax.random.uniform(key_list[2], (1, 1, COLS), jnp.float32, log_low, log_high))
    values = jnp.clip(jax.random.normal(key_list[0], (N_REP, BS, COLS), jnp.float32), -4.0, 4.0)
    scaled = values * row_scale * col_scale * N_REP ** (-0.5)
    return jnp.clip(scaled, -12.0, 12.0).astype(jnp.bfloat16)


def draw_roots(key, part):
    key_list = jax.random.split(jax.random.fold_in(key, 23), 2)
    full_shape = (N_REP, N_SHARD, 2, BS, BS)
    diagonal = jnp.exp(jax.random.uniform(key_list[0], (N_REP, N_SHARD, 2, BS, 1), jnp.float32, math.log(0.25), math.log(0.5)))
    jitter = 0.004 * jnp.clip(jax.random.normal(key_list[1], full_shape, jnp.float32), -4.0, 4.0)
    identity = (jnp.arange(BS)[:, None] == jnp.arange(BS)[None, :]).astype(jnp.float32)
    return (jitter + diagonal * identity).astype(jnp.bfloat16)


def draw_owner_plan(key, part):
    key_list = jax.random.split(jax.random.fold_in(key, 37), N_REP)

    def owner_row(subkey):
        return jax.random.permutation(subkey, N_SHARD)[:BPR]
    return jax.vmap(owner_row)(key_list).astype(jnp.int32)


def draw_refresh(key, part):
    key_list = jax.random.split(jax.random.fold_in(key, 41), N_REP)

    def refresh_row(subkey):
        key_first, second = jax.random.split(subkey)
        chosen = jax.random.permutation(key_first, BPR)[:REFRESH]
        side_bits = jax.random.randint(second, (REFRESH,), 0, 2)
        return 2 * chosen + side_bits
    return jax.vmap(refresh_row)(key_list).astype(jnp.int32)


def setup_inputs(seed: int = 0) -> dict:
    keys = jax.random.split(jax.random.key(seed), 5)
    return {
        "grad_parts": draw_grad_parts(jax.random.fold_in(keys[4], 71), 0),
        "owner_plan": draw_owner_plan(jax.random.fold_in(keys[4], 71), 0),
        "refresh": draw_refresh(jax.random.fold_in(keys[4], 71), 0),
        "roots": draw_roots(jax.random.fold_in(keys[4], 71), 0),
    }


damping = 0.1

def product(first_mat, second_mat):
    return jnp.dot(first_mat, second_mat, precision=lax.Precision.HIGHEST, preferred_element_type=jnp.float32)

def inverse_root(statistic):
    matrix_size = statistic.shape[0]
    identity = jnp.eye(matrix_size, dtype=jnp.float32)
    damped = statistic + (damping * jnp.trace(statistic) / matrix_size + 1e-06) * identity
    norm_scale = 2.5 / jnp.sqrt(jnp.sum(damped * damped))
    current = identity * jnp.sqrt(jnp.sqrt(norm_scale))
    moment = damped * norm_scale
    for repeat in range(NEWTON):
        factor = (5.0 * identity - moment) * 0.25
        current = product(current, factor)
        square = product(factor, factor)
        moment = product(square, product(square, moment))
    return current.astype(jnp.bfloat16)

def reference(grad_parts, owner_plan, refresh, roots):
    summed = lax.optimization_barrier(jnp.sum(grad_parts.astype(jnp.float32), axis=0))
    full_grad = summed.astype(jnp.bfloat16)
    block_count = N_REP * BPR
    all_blocks = full_grad.reshape(BS, block_count, BS).transpose(1, 0, 2)
    replica_of = jnp.arange(block_count, dtype=jnp.int32) // BPR
    local_of = jnp.arange(block_count, dtype=jnp.int32) % BPR
    owner_of = owner_plan.reshape(-1).astype(jnp.int32)
    chosen = refresh[replica_of]

    def per_block(packed):
        grad_block, replica_id, owner_id, local_id, refresh_row = packed
        stored = roots[replica_id, owner_id]
        left_stat = jnp.dot(grad_block, grad_block.T, preferred_element_type=jnp.float32)
        right_stat = jnp.dot(grad_block.T, grad_block, preferred_element_type=jnp.float32)
        left_new = jnp.any(refresh_row == 2 * local_id)
        right_new = jnp.any(refresh_row == 2 * local_id + 1)
        root_left = lax.cond(left_new, lambda: inverse_root(left_stat), lambda: stored[0])
        root_right = lax.cond(right_new, lambda: inverse_root(right_stat), lambda: stored[1])
        left_part = jnp.dot(root_left, grad_block, preferred_element_type=jnp.float32).astype(jnp.bfloat16)
        precon = jnp.dot(left_part, root_right, preferred_element_type=jnp.float32)
        values = grad_block.astype(jnp.float32)
        graft_scale = jnp.sqrt((jnp.mean(values * values) + 1e-06) / (jnp.mean(precon * precon) + 1e-06))
        return (precon * graft_scale).astype(jnp.bfloat16)
    updates = lax.map(per_block, (all_blocks, replica_of, owner_of, local_of, chosen))
    return updates.transpose(1, 0, 2).reshape(BS, block_count * BS)
```

```python
import functools

import jax
import jax.numpy as jnp
from jax import lax
from jax.experimental import pallas as pl
from jax.experimental.pallas import tpu as pltpu
from jax.sharding import PartitionSpec as P

damping = 0.1
MESH = pl.DeviceIdType.MESH
F32 = jnp.float32
BF16 = jnp.bfloat16


def dot(a, b):
    return jnp.dot(a.astype(BF16), b.astype(BF16), preferred_element_type=F32)


def total(x):
    return jnp.sum(jnp.sum(x, axis=0, keepdims=True), axis=1, keepdims=True)


def inverse_root(stat, trace):
    n = stat.shape[0]
    row = lax.broadcasted_iota(jnp.int32, (n, n), 0)
    col = lax.broadcasted_iota(jnp.int32, (n, n), 1)
    eye = row == col
    damped = stat + jnp.where(eye, damping * trace / n + 1e-06, 0.0)
    scale = 2.5 / jnp.sqrt(total(damped * damped))
    moment = damped * scale
    square = dot(moment, moment)
    q = jnp.where(eye, 25.0 / 16.0, 0.0) - 0.625 * moment + 0.0625 * square
    fm = 1.25 * moment - 0.25 * square
    qb = q.astype(BF16)
    tail = dot(dot(fm, qb), qb)
    root = jnp.where(eye, 25.0 / 16.0, 0.0) - 0.3125 * moment - 0.25 * tail
    return (root * jnp.sqrt(jnp.sqrt(scale))).astype(BF16)


def kernel(
    reps, shards, chunks,
    owner, refresh, g_hbm, roots_hbm, out,
    g, roots, rin, lin, rout, lout, acc, full, outb, gbuf, ubuf, back,
    load_sem, rs, rr, ls, lr, a_s, a_r, b_s, b_r,
):
    me = lax.axis_index("shard")
    z = lax.axis_index("rep")
    blocks, _, width = full.shape
    rows_dev = g.shape[0]
    step = rows_dev // chunks
    cols = blocks * width

    load_g = pltpu.make_async_copy(g_hbm, g, load_sem.at[0])
    load_roots = pltpu.make_async_copy(roots_hbm, roots, load_sem.at[1])
    load_g.start()
    load_roots.start()

    barrier = pltpu.get_barrier_semaphore()
    for t in range(1, shards):
        pl.semaphore_signal(
            barrier, inc=1, device_id=(lax.rem(me + t, shards), z), device_id_type=MESH
        )

    @pl.when(z > 0)
    def _():
        pl.semaphore_signal(barrier, inc=1, device_id=(me, z - 1), device_id_type=MESH)

    @pl.when(z < reps - 1)
    def _():
        pl.semaphore_signal(barrier, inc=1, device_id=(me, z + 1), device_id_type=MESH)

    peers = shards - 1 + jnp.where(z > 0, 1, 0) + jnp.where(z < reps - 1, 1, 0)
    pl.semaphore_wait(barrier, peers)

    load_g.wait()

    def rows(k):
        return pl.ds(k * step, step)

    def piece(d, k):
        return g.at[rows(k), pl.ds(pl.multiple_of(d * cols, 128), cols)]

    def right(k, dist, first):
        return pltpu.make_async_remote_copy(
            src_ref=piece(z + dist, k) if first else rout.at[k, dist - 1],
            dst_ref=rin.at[k, dist - 1],
            send_sem=rs.at[k, dist - 1],
            recv_sem=rr.at[k, dist - 1],
            device_id=(me, z + 1),
            device_id_type=MESH,
        )

    def left(k, dist, first):
        return pltpu.make_async_remote_copy(
            src_ref=piece(z - dist, k) if first else lout.at[k, dist - 1],
            dst_ref=lin.at[k, dist - 1],
            send_sem=ls.at[k, dist - 1],
            recv_sem=lr.at[k, dist - 1],
            device_id=(me, z - 1),
            device_id_type=MESH,
        )

    def arrived(buffer, sem, k, slot):
        pltpu.make_async_copy(buffer.at[k, slot], buffer.at[k, slot], sem.at[k, slot]).wait()

    @pl.when(z == 0)
    def _():
        for k in range(chunks):
            for dist in range(reps - 1, 0, -1):
                right(k, dist, True).start()

    @pl.when(z == reps - 1)
    def _():
        for k in range(chunks):
            for dist in range(reps - 1, 0, -1):
                left(k, dist, True).start()

    def slot_block(o):
        def pick(b, found):
            return jnp.where(owner[0, b] == o, b, found)

        return lax.fori_loop(0, blocks, pick, 0, unroll=blocks <= 8)

    def spread(k, t):
        return pltpu.make_async_remote_copy(
            src_ref=outb.at[k, t],
            dst_ref=gbuf.at[me, rows(k)],
            send_sem=a_s.at[k, t],
            recv_sem=a_r.at[k, t],
            device_id=(lax.rem(me + t, shards), z),
            device_id_type=MESH,
        )

    picks = [slot_block(lax.rem(me + t, shards)) for t in range(shards)]

    for k in range(chunks):
        for dist in range(reps - 2, 0, -1):

            @pl.when(jnp.logical_and(z > 0, z + dist <= reps - 1))
            def _():
                arrived(rin, rr, k, dist)
                mine = piece(z + dist, k)[...].astype(F32)
                rout[k, dist - 1] = (rin[k, dist].astype(F32) + mine).astype(BF16)
                right(k, dist, False).start()

            @pl.when(jnp.logical_and(z < reps - 1, z - dist >= 0))
            def _():
                arrived(lin, lr, k, dist)
                mine = piece(z - dist, k)[...].astype(F32)
                lout[k, dist - 1] = (lin[k, dist].astype(F32) + mine).astype(BF16)
                left(k, dist, False).start()

        acc[...] = piece(z, k)[...].astype(F32)

        @pl.when(z > 0)
        def _():
            arrived(rin, rr, k, 0)
            acc[...] += rin[k, 0].astype(F32)

        @pl.when(z < reps - 1)
        def _():
            arrived(lin, lr, k, 0)
            acc[...] += lin[k, 0].astype(F32)

        for b in range(blocks):
            full[b] = acc[:, b * width : (b + 1) * width].astype(BF16)
        for t in range(1, shards):
            outb[k, t] = full[picks[t]]
            spread(k, t).start()
        gbuf[me, k * step : (k + 1) * step] = full[picks[0]]

    load_roots.wait()
    for k in range(chunks):
        for t in range(1, shards):
            spread(k, t).wait_recv()

    size = shards * rows_dev
    if rows_dev % 16 == 0:
        grad = gbuf[...].reshape(size, width)
    else:
        grad = jnp.concatenate([gbuf[s].astype(F32) for s in range(shards)], axis=0).astype(BF16)
    values = grad.astype(F32)
    trace = total(values * values)
    mine = picks[0]
    left_new = jnp.int32(0)
    right_new = jnp.int32(0)
    for i in range(refresh.shape[1]):
        left_new += jnp.where(refresh[0, i] == 2 * mine, 1, 0)
        right_new += jnp.where(refresh[0, i] == 2 * mine + 1, 1, 0)
    left_stat = lax.dot_general(
        grad, grad, (((1,), (1,)), ((), ())), preferred_element_type=F32
    )
    right_stat = lax.dot_general(
        grad, grad, (((0,), (0,)), ((), ())), preferred_element_type=F32
    )
    new_root = inverse_root(jnp.where(right_new > 0, right_stat, left_stat), trace)
    root_left = jnp.where(left_new > 0, new_root, roots[0])
    root_right = jnp.where(right_new > 0, new_root, roots[1])
    precon = dot(dot(root_left, grad), root_right)
    count = size * width
    graft = jnp.sqrt((trace / count + 1e-06) / (total(precon * precon) / count + 1e-06))
    update = precon * graft
    if rows_dev % 16 == 0:
        ubuf[...] = update.astype(BF16).reshape(ubuf.shape)
    else:
        for s in range(shards):
            ubuf[s] = update[s * rows_dev : (s + 1) * rows_dev].astype(BF16)

    def give(t):
        return pltpu.make_async_remote_copy(
            src_ref=ubuf.at[lax.rem(me + t, shards)],
            dst_ref=back.at[me],
            send_sem=b_s.at[t],
            recv_sem=b_r.at[t],
            device_id=(lax.rem(me + t, shards), z),
            device_id_type=MESH,
        )

    for t in range(1, shards):
        give(t).start()
    back[me] = ubuf[me]
    for t in range(1, shards):
        give(t).wait_recv()
    for b in range(blocks):
        out[:, b * width : (b + 1) * width] = back[owner[0, b]]

    for t in range(1, shards):
        give(t).wait_send()
        for k in range(chunks):
            spread(k, t).wait_send()
    for k in range(chunks):
        for dist in range(1, reps):

            @pl.when(z + dist <= reps - 1)
            def _():
                right(k, dist, False).wait_send()

            @pl.when(z - dist >= 0)
            def _():
                left(k, dist, False).wait_send()


def local(grad_parts, owner_plan, refresh, roots):
    shards = lax.axis_size("shard")
    reps = lax.axis_size("rep")
    _, rows_dev, all_cols = grad_parts.shape
    width = roots.shape[-1]
    blocks = owner_plan.shape[-1]
    cols = blocks * width
    chunks = max(1, min(4, rows_dev // 16))
    step = rows_dev // chunks
    hops = max(1, reps - 1)
    dma = pltpu.SemaphoreType.DMA
    anywhere = pl.BlockSpec(memory_space=pl.ANY)
    scalars = pl.BlockSpec(memory_space=pltpu.SMEM)
    return pl.pallas_call(
        functools.partial(kernel, reps, shards, chunks),
        out_shape=jax.ShapeDtypeStruct((rows_dev, cols), BF16),
        in_specs=[scalars, scalars, anywhere, anywhere],
        out_specs=pl.BlockSpec(memory_space=pltpu.VMEM),
        scratch_shapes=[
            pltpu.VMEM((rows_dev, all_cols), BF16),
            pltpu.VMEM((2, width, width), BF16),
            pltpu.VMEM((chunks, hops, step, cols), BF16),
            pltpu.VMEM((chunks, hops, step, cols), BF16),
            pltpu.VMEM((chunks, hops, step, cols), BF16),
            pltpu.VMEM((chunks, hops, step, cols), BF16),
            pltpu.VMEM((step, cols), F32),
            pltpu.VMEM((blocks, step, width), BF16),
            pltpu.VMEM((chunks, shards, step, width), BF16),
            pltpu.VMEM((shards, rows_dev, width), BF16),
            pltpu.VMEM((shards, rows_dev, width), BF16),
            pltpu.VMEM((shards, rows_dev, width), BF16),
            dma((2,)),
            dma((chunks, hops)),
            dma((chunks, hops)),
            dma((chunks, hops)),
            dma((chunks, hops)),
            dma((chunks, shards)),
            dma((chunks, shards)),
            dma((shards,)),
            dma((shards,)),
        ],
        compiler_params=pltpu.CompilerParams(
            collective_id=0, has_side_effects=True, vmem_limit_bytes=60 * 1024 * 1024
        ),
    )(owner_plan, refresh, grad_parts[0], roots[0, 0])


def solution(mesh):
    placed = (
        P("rep", "shard", None),
        P("rep", None),
        P("rep", None),
        P("rep", "shard", None, None, None),
    )
    return jax.shard_map(
        local, mesh=mesh, in_specs=placed, out_specs=P("shard", "rep"), check_vma=False
    )
```

```python
import functools

import jax
import jax.numpy as jnp
from jax import lax
from jax.experimental import pallas as pl
from jax.experimental.pallas import tpu as pltpu
from jax.sharding import PartitionSpec as P

damping = 0.1
MESH = pl.DeviceIdType.MESH
F32 = jnp.float32
BF16 = jnp.bfloat16


def dot(a, b):
    return jnp.dot(a.astype(BF16), b.astype(BF16), preferred_element_type=F32)


def total(x):
    return jnp.sum(jnp.sum(x, axis=0, keepdims=True), axis=1, keepdims=True)


def inverse_root(stat, trace):
    n = stat.shape[0]
    row = lax.broadcasted_iota(jnp.int32, (n, n), 0)
    col = lax.broadcasted_iota(jnp.int32, (n, n), 1)
    eye = row == col
    damped = stat + jnp.where(eye, damping * trace / n + 1e-06, 0.0)
    scale = 2.5 / jnp.sqrt(total(damped * damped))
    moment = damped * scale
    square = dot(moment, moment)
    q = jnp.where(eye, 25.0 / 16.0, 0.0) - 0.625 * moment + 0.0625 * square
    fm = 1.25 * moment - 0.25 * square
    qb = q.astype(BF16)
    tail = dot(dot(fm, qb), qb)
    root = jnp.where(eye, 25.0 / 16.0, 0.0) - 0.3125 * moment - 0.25 * tail
    return (root * jnp.sqrt(jnp.sqrt(scale))).astype(BF16)


def kernel(
    reps, shards, chunks,
    owner, refresh, g_hbm, roots_hbm, out,
    g, roots, rin, lin, rout, lout, acc, full, outb, gbuf, ubuf, back,
    load_sem, rs, rr, ls, lr, a_s, a_r, b_s, b_r,
):
    me = lax.axis_index("shard")
    z = lax.axis_index("rep")
    blocks, _, width = full.shape
    rows_dev = g.shape[0]
    step = rows_dev // chunks
    cols = blocks * width

    load_g = pltpu.make_async_copy(g_hbm, g, load_sem.at[0])
    load_roots = pltpu.make_async_copy(roots_hbm, roots, load_sem.at[1])
    load_g.start()
    load_roots.start()

    barrier = pltpu.get_barrier_semaphore()
    for t in range(1, shards):
        pl.semaphore_signal(
            barrier, inc=1, device_id=(lax.rem(me + t, shards), z), device_id_type=MESH
        )

    @pl.when(z > 0)
    def _():
        pl.semaphore_signal(barrier, inc=1, device_id=(me, z - 1), device_id_type=MESH)

    @pl.when(z < reps - 1)
    def _():
        pl.semaphore_signal(barrier, inc=1, device_id=(me, z + 1), device_id_type=MESH)

    peers = shards - 1 + jnp.where(z > 0, 1, 0) + jnp.where(z < reps - 1, 1, 0)
    pl.semaphore_wait(barrier, peers)

    load_g.wait()

    def rows(k):
        return pl.ds(k * step, step)

    def piece(d, k):
        return g.at[rows(k), pl.ds(pl.multiple_of(d * cols, 128), cols)]

    def right(k, dist, first):
        return pltpu.make_async_remote_copy(
            src_ref=piece(z + dist, k) if first else rout.at[k, dist - 1],
            dst_ref=rin.at[k, dist - 1],
            send_sem=rs.at[k, dist - 1],
            recv_sem=rr.at[k, dist - 1],
            device_id=(me, z + 1),
            device_id_type=MESH,
        )

    def left(k, dist, first):
        return pltpu.make_async_remote_copy(
            src_ref=piece(z - dist, k) if first else lout.at[k, dist - 1],
            dst_ref=lin.at[k, dist - 1],
            send_sem=ls.at[k, dist - 1],
            recv_sem=lr.at[k, dist - 1],
            device_id=(me, z - 1),
            device_id_type=MESH,
        )

    def arrived(buffer, sem, k, slot):
        pltpu.make_async_copy(buffer.at[k, slot], buffer.at[k, slot], sem.at[k, slot]).wait()

    @pl.when(z == 0)
    def _():
        for dist in range(reps - 1, 0, -1):
            for k in range(chunks):
                right(k, dist, True).start()

    @pl.when(z == reps - 1)
    def _():
        for dist in range(reps - 1, 0, -1):
            for k in range(chunks):
                left(k, dist, True).start()

    def slot_block(o):
        def pick(b, found):
            return jnp.where(owner[0, b] == o, b, found)

        return lax.fori_loop(0, blocks, pick, 0, unroll=blocks <= 8)

    def spread(k, t):
        return pltpu.make_async_remote_copy(
            src_ref=outb.at[k, t],
            dst_ref=gbuf.at[me, rows(k)],
            send_sem=a_s.at[k, t],
            recv_sem=a_r.at[k, t],
            device_id=(lax.rem(me + t, shards), z),
            device_id_type=MESH,
        )

    picks = [slot_block(lax.rem(me + t, shards)) for t in range(shards)]

    for dist in range(reps - 2, 0, -1):
        for k in range(chunks):

            @pl.when(jnp.logical_and(z > 0, z + dist <= reps - 1))
            def _():
                arrived(rin, rr, k, dist)
                mine = piece(z + dist, k)[...].astype(F32)
                rout[k, dist - 1] = (rin[k, dist].astype(F32) + mine).astype(BF16)
                right(k, dist, False).start()

            @pl.when(jnp.logical_and(z < reps - 1, z - dist >= 0))
            def _():
                arrived(lin, lr, k, dist)
                mine = piece(z - dist, k)[...].astype(F32)
                lout[k, dist - 1] = (lin[k, dist].astype(F32) + mine).astype(BF16)
                left(k, dist, False).start()

    for k in range(chunks):
        acc[...] = piece(z, k)[...].astype(F32)

        @pl.when(z > 0)
        def _():
            arrived(rin, rr, k, 0)
            acc[...] += rin[k, 0].astype(F32)

        @pl.when(z < reps - 1)
        def _():
            arrived(lin, lr, k, 0)
            acc[...] += lin[k, 0].astype(F32)

        for b in range(blocks):
            full[b] = acc[:, b * width : (b + 1) * width].astype(BF16)
        for t in range(1, shards):
            outb[k, t] = full[picks[t]]
            spread(k, t).start()
        gbuf[me, k * step : (k + 1) * step] = full[picks[0]]

    load_roots.wait()
    for k in range(chunks):
        for t in range(1, shards):
            spread(k, t).wait_recv()

    size = shards * rows_dev
    if rows_dev % 16 == 0:
        grad = gbuf[...].reshape(size, width)
    else:
        grad = jnp.concatenate([gbuf[s].astype(F32) for s in range(shards)], axis=0).astype(BF16)
    values = grad.astype(F32)
    trace = total(values * values)
    mine = picks[0]
    left_new = jnp.int32(0)
    right_new = jnp.int32(0)
    for i in range(refresh.shape[1]):
        left_new += jnp.where(refresh[0, i] == 2 * mine, 1, 0)
        right_new += jnp.where(refresh[0, i] == 2 * mine + 1, 1, 0)
    left_stat = lax.dot_general(
        grad, grad, (((1,), (1,)), ((), ())), preferred_element_type=F32
    )
    right_stat = lax.dot_general(
        grad, grad, (((0,), (0,)), ((), ())), preferred_element_type=F32
    )
    new_root = inverse_root(jnp.where(right_new > 0, right_stat, left_stat), trace)
    root_left = jnp.where(left_new > 0, new_root, roots[0])
    root_right = jnp.where(right_new > 0, new_root, roots[1])
    precon = dot(dot(root_left, grad), root_right)
    count = size * width
    graft = jnp.sqrt((trace / count + 1e-06) / (total(precon * precon) / count + 1e-06))
    update = precon * graft
    if rows_dev % 16 == 0:
        ubuf[...] = update.astype(BF16).reshape(ubuf.shape)
    else:
        for s in range(shards):
            ubuf[s] = update[s * rows_dev : (s + 1) * rows_dev].astype(BF16)

    def give(t):
        return pltpu.make_async_remote_copy(
            src_ref=ubuf.at[lax.rem(me + t, shards)],
            dst_ref=back.at[me],
            send_sem=b_s.at[t],
            recv_sem=b_r.at[t],
            device_id=(lax.rem(me + t, shards), z),
            device_id_type=MESH,
        )

    for t in range(1, shards):
        give(t).start()
    back[me] = ubuf[me]
    for t in range(1, shards):
        give(t).wait_recv()
    for b in range(blocks):
        out[:, b * width : (b + 1) * width] = back[owner[0, b]]

    for t in range(1, shards):
        give(t).wait_send()
        for k in range(chunks):
            spread(k, t).wait_send()
    for k in range(chunks):
        for dist in range(1, reps):

            @pl.when(z + dist <= reps - 1)
            def _():
                right(k, dist, False).wait_send()

            @pl.when(z - dist >= 0)
            def _():
                left(k, dist, False).wait_send()


def local(grad_parts, owner_plan, refresh, roots):
    shards = lax.axis_size("shard")
    reps = lax.axis_size("rep")
    _, rows_dev, all_cols = grad_parts.shape
    width = roots.shape[-1]
    blocks = owner_plan.shape[-1]
    cols = blocks * width
    chunks = max(1, min(4, rows_dev // 16))
    step = rows_dev // chunks
    hops = max(1, reps - 1)
    dma = pltpu.SemaphoreType.DMA
    anywhere = pl.BlockSpec(memory_space=pl.ANY)
    scalars = pl.BlockSpec(memory_space=pltpu.SMEM)
    return pl.pallas_call(
        functools.partial(kernel, reps, shards, chunks),
        out_shape=jax.ShapeDtypeStruct((rows_dev, cols), BF16),
        in_specs=[scalars, scalars, anywhere, anywhere],
        out_specs=pl.BlockSpec(memory_space=pltpu.VMEM),
        scratch_shapes=[
            pltpu.VMEM((rows_dev, all_cols), BF16),
            pltpu.VMEM((2, width, width), BF16),
            pltpu.VMEM((chunks, hops, step, cols), BF16),
            pltpu.VMEM((chunks, hops, step, cols), BF16),
            pltpu.VMEM((chunks, hops, step, cols), BF16),
            pltpu.VMEM((chunks, hops, step, cols), BF16),
            pltpu.VMEM((step, cols), F32),
            pltpu.VMEM((blocks, step, width), BF16),
            pltpu.VMEM((chunks, shards, step, width), BF16),
            pltpu.VMEM((shards, rows_dev, width), BF16),
            pltpu.VMEM((shards, rows_dev, width), BF16),
            pltpu.VMEM((shards, rows_dev, width), BF16),
            dma((2,)),
            dma((chunks, hops)),
            dma((chunks, hops)),
            dma((chunks, hops)),
            dma((chunks, hops)),
            dma((chunks, shards)),
            dma((chunks, shards)),
            dma((shards,)),
            dma((shards,)),
        ],
        compiler_params=pltpu.CompilerParams(
            collective_id=0, has_side_effects=True, vmem_limit_bytes=60 * 1024 * 1024
        ),
    )(owner_plan, refresh, grad_parts[0], roots[0, 0])


def solution(mesh):
    placed = (
        P("rep", "shard", None),
        P("rep", None),
        P("rep", None),
        P("rep", "shard", None, None, None),
    )
    return jax.shard_map(
        local, mesh=mesh, in_specs=placed, out_specs=P("shard", "rep"), check_vma=False
    )
```

```python
import functools

import jax
import jax.numpy as jnp
from jax import lax
from jax.experimental import pallas as pl
from jax.experimental.pallas import tpu as pltpu
from jax.sharding import PartitionSpec as P

damping = 0.1
MESH = pl.DeviceIdType.MESH
F32 = jnp.float32
BF16 = jnp.bfloat16


def dot(a, b):
    return jnp.dot(a.astype(BF16), b.astype(BF16), preferred_element_type=F32)


def total(x):
    return jnp.sum(jnp.sum(x, axis=0, keepdims=True), axis=1, keepdims=True)


def inverse_root(stat, trace):
    n = stat.shape[0]
    row = lax.broadcasted_iota(jnp.int32, (n, n), 0)
    col = lax.broadcasted_iota(jnp.int32, (n, n), 1)
    eye = row == col
    damped = stat + jnp.where(eye, damping * trace / n + 1e-06, 0.0)
    scale = 2.5 / jnp.sqrt(total(damped * damped))
    moment = damped * scale
    square = dot(moment, moment)
    q = jnp.where(eye, 25.0 / 16.0, 0.0) - 0.625 * moment + 0.0625 * square
    fm = 1.25 * moment - 0.25 * square
    qb = q.astype(BF16)
    tail = dot(dot(fm, qb), qb)
    root = jnp.where(eye, 25.0 / 16.0, 0.0) - 0.3125 * moment - 0.25 * tail
    return (root * jnp.sqrt(jnp.sqrt(scale))).astype(BF16)


def mix(a, t, n):
    if n & (n - 1):
        return lax.rem(a + t, n)
    out, bit = a, 1
    while bit < n:
        if t & bit:
            out = out + bit - 2 * bit * lax.rem(a // bit, 2)
        bit *= 2
    return out


def unmix(a, t, n):
    return lax.rem(a + n - t, n) if n & (n - 1) else mix(a, t, n)


def whole_block(ref, rows_dev):
    shards, _, width = ref.shape
    if rows_dev % 16 == 0:
        return ref[...].reshape(shards * rows_dev, width)
    return jnp.concatenate([ref[s].astype(F32) for s in range(shards)], axis=0).astype(BF16)


def precondition(shards, rows_dev, refresh, mine, gbuf, roots, ubuf, landed_roots):
    grad = whole_block(gbuf, rows_dev)
    size, width = grad.shape
    values = grad.astype(F32)
    trace = total(values * values)
    left_new = jnp.int32(0)
    right_new = jnp.int32(0)
    for i in range(refresh.shape[1]):
        left_new += jnp.where(refresh[0, i] == 2 * mine, 1, 0)
        right_new += jnp.where(refresh[0, i] == 2 * mine + 1, 1, 0)
    left_stat = lax.dot_general(
        grad, grad, (((1,), (1,)), ((), ())), preferred_element_type=F32
    )
    right_stat = lax.dot_general(
        grad, grad, (((0,), (0,)), ((), ())), preferred_element_type=F32
    )
    new_root = inverse_root(jnp.where(right_new > 0, right_stat, left_stat), trace)
    landed_roots()
    root_left = jnp.where(left_new > 0, new_root, whole_block(roots.at[0], rows_dev))
    root_right = jnp.where(right_new > 0, new_root, whole_block(roots.at[1], rows_dev))
    precon = dot(dot(root_left, grad), root_right)
    count = size * width
    graft = jnp.sqrt((trace / count + 1e-06) / (total(precon * precon) / count + 1e-06))
    update = precon * graft
    if rows_dev % 16 == 0:
        ubuf[...] = update.astype(BF16).reshape(ubuf.shape)
    else:
        for s in range(shards):
            ubuf[s] = update[s * rows_dev : (s + 1) * rows_dev].astype(BF16)


def kernel(
    reps, shards, chunks,
    owner, refresh, g_hbm, roots_hbm, out,
    g, rin, lin, rout, lout, acc, full, gbuf, ubuf, slices, chosen, roots,
    load_sem, rs, rr, ls, lr, a_s, a_r, b_s, b_r, c_s, c_r, d_s, d_r,
):
    me = lax.axis_index("shard")
    z = lax.axis_index("rep")
    _, blocks, step, width = full.shape
    rows_dev = g.shape[0]
    cols = blocks * width
    per = shards // blocks
    mine = me // per
    is_home = lax.rem(me, per) == 0
    not_home = lax.rem(me, per) > 0

    load_g = pltpu.make_async_copy(g_hbm, g, load_sem.at[0])
    load_g.start()
    keep = pltpu.make_async_copy(
        roots_hbm.at[:, pl.ds(pl.multiple_of(me * rows_dev, 8), rows_dev)],
        slices.at[me],
        load_sem.at[1],
    )
    keep.start()

    barrier = pltpu.get_barrier_semaphore()
    for t in range(1, shards):
        pl.semaphore_signal(
            barrier, inc=1, device_id=(lax.rem(me + t, shards), z), device_id_type=MESH
        )

    @pl.when(z > 0)
    def _():
        pl.semaphore_signal(barrier, inc=1, device_id=(me, z - 1), device_id_type=MESH)

    @pl.when(z < reps - 1)
    def _():
        pl.semaphore_signal(barrier, inc=1, device_id=(me, z + 1), device_id_type=MESH)

    peers = shards - 1 + jnp.where(z > 0, 1, 0) + jnp.where(z < reps - 1, 1, 0)
    pl.semaphore_wait(barrier, peers)

    def cut(t):
        peer = mix(me, t, shards)
        return pltpu.make_async_remote_copy(
            src_ref=roots_hbm.at[:, pl.ds(pl.multiple_of(peer * rows_dev, 8), rows_dev)],
            dst_ref=slices.at[me],
            send_sem=c_s.at[t],
            recv_sem=c_r.at[me],
            device_id=(peer, z),
            device_id_type=MESH,
        )

    load_g.wait()

    def rows(k):
        return pl.ds(k * step, step)

    def piece(d, k):
        return g.at[rows(k), pl.ds(pl.multiple_of(d * cols, 128), cols)]

    def right(k, dist, first):
        return pltpu.make_async_remote_copy(
            src_ref=piece(z + dist, k) if first else rout.at[k, dist - 1],
            dst_ref=rin.at[k, dist - 1],
            send_sem=rs.at[k, dist - 1],
            recv_sem=rr.at[k, dist - 1],
            device_id=(me, z + 1),
            device_id_type=MESH,
        )

    def left(k, dist, first):
        return pltpu.make_async_remote_copy(
            src_ref=piece(z - dist, k) if first else lout.at[k, dist - 1],
            dst_ref=lin.at[k, dist - 1],
            send_sem=ls.at[k, dist - 1],
            recv_sem=lr.at[k, dist - 1],
            device_id=(me, z - 1),
            device_id_type=MESH,
        )

    def arrived(buffer, sem, k, slot):
        pltpu.make_async_copy(buffer.at[k, slot], buffer.at[k, slot], sem.at[k, slot]).wait()

    @pl.when(z == 0)
    def _():
        for dist in range(reps - 1, 0, -1):
            for k in range(chunks):
                right(k, dist, True).start()

    @pl.when(z == reps - 1)
    def _():
        for dist in range(reps - 1, 0, -1):
            for k in range(chunks):
                left(k, dist, True).start()

    for t in range(shards - 1, 0, -1):
        cut(t).start()

    def to_home(j, src, dst, send, recv):
        return pltpu.make_async_remote_copy(
            src_ref=src,
            dst_ref=dst,
            send_sem=send,
            recv_sem=recv,
            device_id=(mix(mine, j, blocks) * per, z),
            device_id_type=MESH,
        )

    def lend(j):
        return to_home(j, chosen.at[j], roots.at[:, me], d_s.at[j], d_r.at[me])

    def spread(k, j):
        b = mix(mine, j, blocks)
        return to_home(j, full.at[k, b], gbuf.at[me, rows(k)], a_s.at[k, j], a_r.at[k, me])

    def landed(ref, sem):
        pltpu.make_async_copy(ref, ref, sem).wait()

    for dist in range(reps - 2, 0, -1):
        for k in range(chunks):

            @pl.when(jnp.logical_and(z > 0, z + dist <= reps - 1))
            def _():
                arrived(rin, rr, k, dist)
                mine = piece(z + dist, k)[...].astype(F32)
                rout[k, dist - 1] = (rin[k, dist].astype(F32) + mine).astype(BF16)
                right(k, dist, False).start()

            @pl.when(jnp.logical_and(z < reps - 1, z - dist >= 0))
            def _():
                arrived(lin, lr, k, dist)
                mine = piece(z - dist, k)[...].astype(F32)
                lout[k, dist - 1] = (lin[k, dist].astype(F32) + mine).astype(BF16)
                left(k, dist, False).start()

    keep.wait()
    for t in range(shards - 1, 0, -1):
        peer = unmix(me, t, shards)
        landed(slices.at[peer], c_r.at[peer])
    for j in range(blocks - 1, 0, -1):
        chosen[j] = slices[owner[0, mix(mine, j, blocks)]]
        lend(j).start()

    @pl.when(is_home)
    def _():
        roots[:, me] = slices[owner[0, mine]]

    @pl.when(not_home)
    def _():
        chosen[0] = slices[owner[0, mine]]
        lend(0).start()

    for k in range(chunks):
        acc[...] = piece(z, k)[...].astype(F32)

        @pl.when(z > 0)
        def _():
            arrived(rin, rr, k, 0)
            acc[...] += rin[k, 0].astype(F32)

        @pl.when(z < reps - 1)
        def _():
            arrived(lin, lr, k, 0)
            acc[...] += lin[k, 0].astype(F32)

        for b in range(blocks):
            full[k, b] = acc[:, b * width : (b + 1) * width].astype(BF16)
        for j in range(blocks - 1, 0, -1):
            spread(k, j).start()

        @pl.when(is_home)
        def _():
            gbuf[me, k * step : (k + 1) * step] = full[k, mine]

        @pl.when(not_home)
        def _():
            spread(k, 0).start()

    def give(t):
        peer = mix(me, t, shards)
        return pltpu.make_async_remote_copy(
            src_ref=ubuf.at[peer],
            dst_ref=place(mine),
            send_sem=b_s.at[t],
            recv_sem=b_r.at[mine],
            device_id=(peer, z),
            device_id_type=MESH,
        )

    def place(b):
        return out.at[:, pl.ds(pl.multiple_of(b * width, 128), width)]

    def landed_roots():
        for t in range(shards - 1, 0, -1):
            peer = unmix(me, t, shards)
            landed(roots.at[:, peer], d_r.at[peer])

    put = pltpu.make_async_copy(ubuf.at[me], place(mine), load_sem.at[2])

    @pl.when(is_home)
    def _():
        for k in range(chunks):
            for t in range(shards - 1, 0, -1):
                peer = unmix(me, t, shards)
                landed(gbuf.at[peer, rows(k)], a_r.at[k, peer])
        precondition(shards, rows_dev, refresh, mine, gbuf, roots, ubuf, landed_roots)
        for t in range(shards - 1, 0, -1):
            give(t).start()
        put.start()

    for j in range(blocks - 1, 0, -1):
        b = unmix(mine, j, blocks)
        landed(place(b), b_r.at[b])

    @pl.when(not_home)
    def _():
        landed(place(mine), b_r.at[mine])
        lend(0).wait_send()
        for k in range(chunks):
            spread(k, 0).wait_send()

    @pl.when(is_home)
    def _():
        put.wait()
        for t in range(1, shards):
            give(t).wait_send()

    for t in range(1, shards):
        cut(t).wait_send()
    for j in range(1, blocks):
        lend(j).wait_send()
        for k in range(chunks):
            spread(k, j).wait_send()
    for k in range(chunks):
        for dist in range(1, reps):

            @pl.when(z + dist <= reps - 1)
            def _():
                right(k, dist, False).wait_send()

            @pl.when(z - dist >= 0)
            def _():
                left(k, dist, False).wait_send()


def local(grad_parts, owner_plan, refresh, roots):
    shards = lax.axis_size("shard")
    reps = lax.axis_size("rep")
    _, rows_dev, all_cols = grad_parts.shape
    width = roots.shape[-1]
    blocks = owner_plan.shape[-1]
    cols = blocks * width
    chunks = max(1, min(4, rows_dev // 16))
    step = rows_dev // chunks
    hops = max(1, reps - 1)
    dma = pltpu.SemaphoreType.DMA
    anywhere = pl.BlockSpec(memory_space=pl.ANY)
    scalars = pl.BlockSpec(memory_space=pltpu.SMEM)
    return pl.pallas_call(
        functools.partial(kernel, reps, shards, chunks),
        out_shape=jax.ShapeDtypeStruct((rows_dev, cols), BF16),
        in_specs=[scalars, scalars, anywhere, anywhere],
        out_specs=anywhere,
        scratch_shapes=[
            pltpu.VMEM((rows_dev, all_cols), BF16),
            pltpu.VMEM((chunks, hops, step, cols), BF16),
            pltpu.VMEM((chunks, hops, step, cols), BF16),
            pltpu.VMEM((chunks, hops, step, cols), BF16),
            pltpu.VMEM((chunks, hops, step, cols), BF16),
            pltpu.VMEM((step, cols), F32),
            pltpu.VMEM((chunks, blocks, step, width), BF16),
            pltpu.VMEM((shards, rows_dev, width), BF16),
            pltpu.VMEM((shards, rows_dev, width), BF16),
            pltpu.VMEM((shards, 2, rows_dev, width), BF16),
            pltpu.VMEM((blocks, 2, rows_dev, width), BF16),
            pltpu.VMEM((2, shards, rows_dev, width), BF16),
            dma((3,)),
            dma((chunks, hops)),
            dma((chunks, hops)),
            dma((chunks, hops)),
            dma((chunks, hops)),
            dma((chunks, blocks)),
            dma((chunks, shards)),
            dma((shards,)),
            dma((blocks,)),
            dma((shards,)),
            dma((shards,)),
            dma((blocks,)),
            dma((shards,)),
        ],
        compiler_params=pltpu.CompilerParams(
            collective_id=0, has_side_effects=True, vmem_limit_bytes=60 * 1024 * 1024
        ),
    )(owner_plan, refresh, grad_parts[0], roots[0, 0])


def solution(mesh):
    placed = (
        P("rep", "shard", None),
        P("rep", None),
        P("rep", None),
        P("rep", "shard", None, None, None),
    )
    return jax.shard_map(
        local, mesh=mesh, in_specs=placed, out_specs=P("shard", "rep"), check_vma=False
    )
```

```python
import functools

import jax
import jax.numpy as jnp
from jax import lax
from jax.experimental import pallas as pl
from jax.experimental.pallas import tpu as pltpu
from jax.sharding import PartitionSpec as P

damping = 0.1
MESH = pl.DeviceIdType.MESH
F32 = jnp.float32
BF16 = jnp.bfloat16


def dot(a, b):
    return jnp.dot(a.astype(BF16), b.astype(BF16), preferred_element_type=F32)


def total(x):
    return jnp.sum(jnp.sum(x, axis=0, keepdims=True), axis=1, keepdims=True)


def inverse_root(stat, trace):
    n = stat.shape[0]
    row = lax.broadcasted_iota(jnp.int32, (n, n), 0)
    col = lax.broadcasted_iota(jnp.int32, (n, n), 1)
    eye = row == col
    damped = stat + jnp.where(eye, damping * trace / n + 1e-06, 0.0)
    scale = 2.5 / jnp.sqrt(total(damped * damped))
    moment = damped * scale
    square = dot(moment, moment)
    q = jnp.where(eye, 25.0 / 16.0, 0.0) - 0.625 * moment + 0.0625 * square
    fm = 1.25 * moment - 0.25 * square
    qb = q.astype(BF16)
    tail = dot(dot(fm, qb), qb)
    root = jnp.where(eye, 25.0 / 16.0, 0.0) - 0.3125 * moment - 0.25 * tail
    return (root * jnp.sqrt(jnp.sqrt(scale))).astype(BF16)


def mix(a, t, n):
    if n & (n - 1):
        return lax.rem(a + t, n)
    out, bit = a, 1
    while bit < n:
        if t & bit:
            out = out + bit - 2 * bit * lax.rem(a // bit, 2)
        bit *= 2
    return out


def unmix(a, t, n):
    return lax.rem(a + n - t, n) if n & (n - 1) else mix(a, t, n)


def whole_block(ref, rows_dev):
    shards, _, width = ref.shape
    if rows_dev % 16 == 0:
        return ref[...].reshape(shards * rows_dev, width)
    return jnp.concatenate([ref[s].astype(F32) for s in range(shards)], axis=0).astype(BF16)


def precondition(shards, rows_dev, refresh, mine, gbuf, roots, ubuf, landed_roots):
    grad = whole_block(gbuf, rows_dev)
    size, width = grad.shape
    values = grad.astype(F32)
    trace = total(values * values)
    left_new = jnp.int32(0)
    right_new = jnp.int32(0)
    for i in range(refresh.shape[1]):
        left_new += jnp.where(refresh[0, i] == 2 * mine, 1, 0)
        right_new += jnp.where(refresh[0, i] == 2 * mine + 1, 1, 0)
    left_stat = lax.dot_general(
        grad, grad, (((1,), (1,)), ((), ())), preferred_element_type=F32
    )
    right_stat = lax.dot_general(
        grad, grad, (((0,), (0,)), ((), ())), preferred_element_type=F32
    )
    new_root = inverse_root(jnp.where(right_new > 0, right_stat, left_stat), trace)
    landed_roots()
    root_left = jnp.where(left_new > 0, new_root, whole_block(roots.at[0], rows_dev))
    root_right = jnp.where(right_new > 0, new_root, whole_block(roots.at[1], rows_dev))
    precon = dot(dot(root_left, grad), root_right)
    count = size * width
    graft = jnp.sqrt((trace / count + 1e-06) / (total(precon * precon) / count + 1e-06))
    update = precon * graft
    if rows_dev % 16 == 0:
        ubuf[...] = update.astype(BF16).reshape(ubuf.shape)
    else:
        for s in range(shards):
            ubuf[s] = update[s * rows_dev : (s + 1) * rows_dev].astype(BF16)


def kernel(
    reps, shards, chunks,
    owner, refresh, g_hbm, roots_hbm, out,
    g, rin, lin, rout, lout, acc, full, gbuf, ubuf, left_cuts, right_cuts, chosen, roots,
    load_sem, rs, rr, ls, lr, a_s, a_r, b_s, b_r, c_s, c_r, d_s, d_r,
):
    me = lax.axis_index("shard")
    z = lax.axis_index("rep")
    _, blocks, step, width = full.shape
    rows_dev = g.shape[0]
    cols = blocks * width
    per = shards // blocks
    mine = me // per
    is_home = lax.rem(me, per) == 0
    not_home = lax.rem(me, per) > 0

    load_g = pltpu.make_async_copy(g_hbm, g, load_sem.at[0])
    load_g.start()
    slices = (left_cuts, right_cuts)
    keep = [
        pltpu.make_async_copy(
            roots_hbm.at[i, pl.ds(pl.multiple_of(me * rows_dev, 8), rows_dev)],
            slices[i].at[me],
            load_sem.at[1 + i],
        )
        for i in range(2)
    ]
    for copy in keep:
        copy.start()

    barrier = pltpu.get_barrier_semaphore()
    for t in range(1, shards):
        pl.semaphore_signal(
            barrier, inc=1, device_id=(lax.rem(me + t, shards), z), device_id_type=MESH
        )

    @pl.when(z > 0)
    def _():
        pl.semaphore_signal(barrier, inc=1, device_id=(me, z - 1), device_id_type=MESH)

    @pl.when(z < reps - 1)
    def _():
        pl.semaphore_signal(barrier, inc=1, device_id=(me, z + 1), device_id_type=MESH)

    peers = shards - 1 + jnp.where(z > 0, 1, 0) + jnp.where(z < reps - 1, 1, 0)
    pl.semaphore_wait(barrier, peers)

    def cut(i, t):
        peer = mix(me, t, shards)
        return pltpu.make_async_remote_copy(
            src_ref=roots_hbm.at[i, pl.ds(pl.multiple_of(peer * rows_dev, 8), rows_dev)],
            dst_ref=slices[i].at[me],
            send_sem=c_s.at[i, t],
            recv_sem=c_r.at[i, me],
            device_id=(peer, z),
            device_id_type=MESH,
        )

    load_g.wait()

    def rows(k):
        return pl.ds(k * step, step)

    def piece(d, k):
        return g.at[rows(k), pl.ds(pl.multiple_of(d * cols, 128), cols)]

    def right(k, dist, first):
        return pltpu.make_async_remote_copy(
            src_ref=piece(z + dist, k) if first else rout.at[k, dist - 1],
            dst_ref=rin.at[k, dist - 1],
            send_sem=rs.at[k, dist - 1],
            recv_sem=rr.at[k, dist - 1],
            device_id=(me, z + 1),
            device_id_type=MESH,
        )

    def left(k, dist, first):
        return pltpu.make_async_remote_copy(
            src_ref=piece(z - dist, k) if first else lout.at[k, dist - 1],
            dst_ref=lin.at[k, dist - 1],
            send_sem=ls.at[k, dist - 1],
            recv_sem=lr.at[k, dist - 1],
            device_id=(me, z - 1),
            device_id_type=MESH,
        )

    def arrived(buffer, sem, k, slot):
        pltpu.make_async_copy(buffer.at[k, slot], buffer.at[k, slot], sem.at[k, slot]).wait()

    @pl.when(z == 0)
    def _():
        for dist in range(reps - 1, 0, -1):
            for k in range(chunks):
                right(k, dist, True).start()

    @pl.when(z == reps - 1)
    def _():
        for dist in range(reps - 1, 0, -1):
            for k in range(chunks):
                left(k, dist, True).start()

    for i in range(2):
        for t in range(shards - 1, 0, -1):
            cut(i, t).start()

    def to_home(j, src, dst, send, recv):
        return pltpu.make_async_remote_copy(
            src_ref=src,
            dst_ref=dst,
            send_sem=send,
            recv_sem=recv,
            device_id=(mix(mine, j, blocks) * per, z),
            device_id_type=MESH,
        )

    def lend(i, j):
        return to_home(j, chosen.at[i, j], roots.at[i, me], d_s.at[i, j], d_r.at[i, me])

    def spread(k, j):
        b = mix(mine, j, blocks)
        return to_home(j, full.at[k, b], gbuf.at[me, rows(k)], a_s.at[k, j], a_r.at[k, me])

    def landed(ref, sem):
        pltpu.make_async_copy(ref, ref, sem).wait()

    def pass_on(i):
        for t in range(shards - 1, 0, -1):
            peer = unmix(me, t, shards)
            landed(slices[i].at[peer], c_r.at[i, peer])
        for j in range(blocks - 1, 0, -1):
            chosen[i, j] = slices[i][owner[0, mix(mine, j, blocks)]]
            lend(i, j).start()

        @pl.when(is_home)
        def _():
            roots[i, me] = slices[i][owner[0, mine]]

        @pl.when(not_home)
        def _():
            chosen[i, 0] = slices[i][owner[0, mine]]
            lend(i, 0).start()

    for copy in keep:
        copy.wait()
    for dist in range(reps - 2, 0, -1):
        if dist == 1:
            pass_on(0)
        for k in range(chunks):

            @pl.when(jnp.logical_and(z > 0, z + dist <= reps - 1))
            def _():
                arrived(rin, rr, k, dist)
                mine = piece(z + dist, k)[...].astype(F32)
                rout[k, dist - 1] = (rin[k, dist].astype(F32) + mine).astype(BF16)
                right(k, dist, False).start()

            @pl.when(jnp.logical_and(z < reps - 1, z - dist >= 0))
            def _():
                arrived(lin, lr, k, dist)
                mine = piece(z - dist, k)[...].astype(F32)
                lout[k, dist - 1] = (lin[k, dist].astype(F32) + mine).astype(BF16)
                left(k, dist, False).start()

    for i in range(1 if reps > 2 else 0, 2):
        pass_on(i)

    for k in range(chunks):
        acc[...] = piece(z, k)[...].astype(F32)

        @pl.when(z > 0)
        def _():
            arrived(rin, rr, k, 0)
            acc[...] += rin[k, 0].astype(F32)

        @pl.when(z < reps - 1)
        def _():
            arrived(lin, lr, k, 0)
            acc[...] += lin[k, 0].astype(F32)

        for b in range(blocks):
            full[k, b] = acc[:, b * width : (b + 1) * width].astype(BF16)
        for j in range(blocks - 1, 0, -1):
            spread(k, j).start()

        @pl.when(is_home)
        def _():
            gbuf[me, k * step : (k + 1) * step] = full[k, mine]

        @pl.when(not_home)
        def _():
            spread(k, 0).start()

    def give(t):
        peer = mix(me, t, shards)
        return pltpu.make_async_remote_copy(
            src_ref=ubuf.at[peer],
            dst_ref=place(mine),
            send_sem=b_s.at[t],
            recv_sem=b_r.at[mine],
            device_id=(peer, z),
            device_id_type=MESH,
        )

    def place(b):
        return out.at[:, pl.ds(pl.multiple_of(b * width, 128), width)]

    def landed_roots():
        for i in range(2):
            for t in range(shards - 1, 0, -1):
                peer = unmix(me, t, shards)
                landed(roots.at[i, peer], d_r.at[i, peer])

    put = pltpu.make_async_copy(ubuf.at[me], place(mine), load_sem.at[3])

    @pl.when(is_home)
    def _():
        for k in range(chunks):
            for t in range(shards - 1, 0, -1):
                peer = unmix(me, t, shards)
                landed(gbuf.at[peer, rows(k)], a_r.at[k, peer])
        precondition(shards, rows_dev, refresh, mine, gbuf, roots, ubuf, landed_roots)
        for t in range(shards - 1, 0, -1):
            give(t).start()
        put.start()

    for j in range(blocks - 1, 0, -1):
        b = unmix(mine, j, blocks)
        landed(place(b), b_r.at[b])

    @pl.when(not_home)
    def _():
        landed(place(mine), b_r.at[mine])
        for i in range(2):
            lend(i, 0).wait_send()
        for k in range(chunks):
            spread(k, 0).wait_send()

    @pl.when(is_home)
    def _():
        put.wait()
        for t in range(1, shards):
            give(t).wait_send()

    for t in range(1, shards):
        for i in range(2):
            cut(i, t).wait_send()
    for j in range(1, blocks):
        for i in range(2):
            lend(i, j).wait_send()
        for k in range(chunks):
            spread(k, j).wait_send()
    for k in range(chunks):
        for dist in range(1, reps):

            @pl.when(z + dist <= reps - 1)
            def _():
                right(k, dist, False).wait_send()

            @pl.when(z - dist >= 0)
            def _():
                left(k, dist, False).wait_send()


def local(grad_parts, owner_plan, refresh, roots):
    shards = lax.axis_size("shard")
    reps = lax.axis_size("rep")
    _, rows_dev, all_cols = grad_parts.shape
    width = roots.shape[-1]
    blocks = owner_plan.shape[-1]
    cols = blocks * width
    chunks = max(1, min(2, rows_dev // 16))
    step = rows_dev // chunks
    hops = max(1, reps - 1)
    dma = pltpu.SemaphoreType.DMA
    anywhere = pl.BlockSpec(memory_space=pl.ANY)
    scalars = pl.BlockSpec(memory_space=pltpu.SMEM)
    return pl.pallas_call(
        functools.partial(kernel, reps, shards, chunks),
        out_shape=jax.ShapeDtypeStruct((rows_dev, cols), BF16),
        in_specs=[scalars, scalars, anywhere, anywhere],
        out_specs=anywhere,
        scratch_shapes=[
            pltpu.VMEM((rows_dev, all_cols), BF16),
            pltpu.VMEM((chunks, hops, step, cols), BF16),
            pltpu.VMEM((chunks, hops, step, cols), BF16),
            pltpu.VMEM((chunks, hops, step, cols), BF16),
            pltpu.VMEM((chunks, hops, step, cols), BF16),
            pltpu.VMEM((step, cols), F32),
            pltpu.VMEM((chunks, blocks, step, width), BF16),
            pltpu.VMEM((shards, rows_dev, width), BF16),
            pltpu.VMEM((shards, rows_dev, width), BF16),
            pltpu.VMEM((shards, rows_dev, width), BF16),
            pltpu.VMEM((shards, rows_dev, width), BF16),
            pltpu.VMEM((2, blocks, rows_dev, width), BF16),
            pltpu.VMEM((2, shards, rows_dev, width), BF16),
            dma((4,)),
            dma((chunks, hops)),
            dma((chunks, hops)),
            dma((chunks, hops)),
            dma((chunks, hops)),
            dma((chunks, blocks)),
            dma((chunks, shards)),
            dma((shards,)),
            dma((blocks,)),
            dma((2, shards)),
            dma((2, shards)),
            dma((2, blocks)),
            dma((2, shards)),
        ],
        compiler_params=pltpu.CompilerParams(
            collective_id=0, has_side_effects=True, vmem_limit_bytes=60 * 1024 * 1024
        ),
    )(owner_plan, refresh, grad_parts[0], roots[0, 0])


def solution(mesh):
    placed = (
        P("rep", "shard", None),
        P("rep", None),
        P("rep", None),
        P("rep", "shard", None, None, None),
    )
    return jax.shard_map(
        local, mesh=mesh, in_specs=placed, out_specs=P("shard", "rep"), check_vma=False
    )
```

```python
import functools

import jax
import jax.numpy as jnp
from jax import lax
from jax.experimental import pallas as pl
from jax.experimental.pallas import tpu as pltpu
from jax.sharding import PartitionSpec as P

damping = 0.1
MESH = pl.DeviceIdType.MESH
F32 = jnp.float32
BF16 = jnp.bfloat16


def dot(a, b):
    return jnp.dot(a.astype(BF16), b.astype(BF16), preferred_element_type=F32)


def total(x):
    return jnp.sum(jnp.sum(x, axis=0, keepdims=True), axis=1, keepdims=True)


def inverse_root(stat, trace):
    n = stat.shape[0]
    row = lax.broadcasted_iota(jnp.int32, (n, n), 0)
    col = lax.broadcasted_iota(jnp.int32, (n, n), 1)
    eye = row == col
    damped = stat + jnp.where(eye, damping * trace / n + 1e-06, 0.0)
    scale = 2.5 / jnp.sqrt(total(damped * damped))
    moment = damped * scale
    square = dot(moment, moment)
    q = jnp.where(eye, 25.0 / 16.0, 0.0) - 0.625 * moment + 0.0625 * square
    fm = 1.25 * moment - 0.25 * square
    qb = q.astype(BF16)
    tail = dot(dot(fm, qb), qb)
    root = jnp.where(eye, 25.0 / 16.0, 0.0) - 0.3125 * moment - 0.25 * tail
    return (root * jnp.sqrt(jnp.sqrt(scale))).astype(BF16)


def mix(a, t, n):
    if n & (n - 1):
        return lax.rem(a + t, n)
    out, bit = a, 1
    while bit < n:
        if t & bit:
            out = out + bit - 2 * bit * lax.rem(a // bit, 2)
        bit *= 2
    return out


def unmix(a, t, n):
    return lax.rem(a + n - t, n) if n & (n - 1) else mix(a, t, n)


def whole_block(ref, rows_dev):
    shards, _, width = ref.shape
    if rows_dev % 16 == 0:
        return ref[...].reshape(shards * rows_dev, width)
    return jnp.concatenate([ref[s].astype(F32) for s in range(shards)], axis=0).astype(BF16)


def precondition(shards, rows_dev, refresh, mine, gbuf, roots, ubuf, landed_roots, gscale, send_rows):
    grad = whole_block(gbuf, rows_dev)
    size, width = grad.shape
    values = grad.astype(F32)
    trace = total(values * values)
    left_new = jnp.int32(0)
    right_new = jnp.int32(0)
    for i in range(refresh.shape[1]):
        left_new += jnp.where(refresh[0, i] == 2 * mine, 1, 0)
        right_new += jnp.where(refresh[0, i] == 2 * mine + 1, 1, 0)
    left_stat = lax.dot_general(
        grad, grad, (((1,), (1,)), ((), ())), preferred_element_type=F32
    )
    right_stat = lax.dot_general(
        grad, grad, (((0,), (0,)), ((), ())), preferred_element_type=F32
    )
    new_root = inverse_root(jnp.where(right_new > 0, right_stat, left_stat), trace)
    landed_roots()
    root_left = jnp.where(left_new > 0, new_root, whole_block(roots.at[0], rows_dev))
    root_right = jnp.where(right_new > 0, new_root, whole_block(roots.at[1], rows_dev))
    left_part = dot(root_left, grad).astype(BF16)
    count = size * width
    squares = jnp.zeros((1, 1), F32)
    group = max(1, shards // 4)
    for start in range(0, shards, group):
        span = group * rows_dev
        precon = dot(left_part[start * rows_dev : start * rows_dev + span], root_right)
        squares += total(precon * precon)
        if rows_dev % 16 == 0:
            ubuf[start : start + group] = precon.astype(BF16).reshape(group, rows_dev, width)
        else:
            for s in range(group):
                ubuf[start + s] = precon[s * rows_dev : (s + 1) * rows_dev].astype(BF16)
        for s in range(start, start + group):
            send_rows(s)
    graft = jnp.sqrt((trace / count + 1e-06) / (squares / count + 1e-06))
    gscale[...] = jnp.broadcast_to(graft, gscale.shape)


def kernel(
    reps, shards, chunks,
    owner, refresh, g_hbm, roots_hbm, out, scales,
    g, rin, lin, rout, lout, acc, full, gbuf, ubuf, left_cuts, right_cuts, chosen, roots, gscale,
    load_sem, rs, rr, ls, lr, a_s, a_r, b_s, b_r, e_s, e_r, c_s, c_r, d_s, d_r,
):
    me = lax.axis_index("shard")
    z = lax.axis_index("rep")
    _, blocks, step, width = full.shape
    rows_dev = g.shape[0]
    cols = blocks * width
    per = shards // blocks
    mine = me // per
    is_home = lax.rem(me, per) == 0
    not_home = lax.rem(me, per) > 0

    load_g = pltpu.make_async_copy(g_hbm, g, load_sem.at[0])
    load_g.start()
    slices = (left_cuts, right_cuts)
    keep = [
        pltpu.make_async_copy(
            roots_hbm.at[i, pl.ds(pl.multiple_of(me * rows_dev, 8), rows_dev)],
            slices[i].at[me],
            load_sem.at[1 + i],
        )
        for i in range(2)
    ]
    for copy in keep:
        copy.start()

    barrier = pltpu.get_barrier_semaphore()
    for t in range(1, shards):
        pl.semaphore_signal(
            barrier, inc=1, device_id=(lax.rem(me + t, shards), z), device_id_type=MESH
        )

    @pl.when(z > 0)
    def _():
        pl.semaphore_signal(barrier, inc=1, device_id=(me, z - 1), device_id_type=MESH)

    @pl.when(z < reps - 1)
    def _():
        pl.semaphore_signal(barrier, inc=1, device_id=(me, z + 1), device_id_type=MESH)

    peers = shards - 1 + jnp.where(z > 0, 1, 0) + jnp.where(z < reps - 1, 1, 0)
    pl.semaphore_wait(barrier, peers)

    def cut(i, t):
        peer = mix(me, t, shards)
        return pltpu.make_async_remote_copy(
            src_ref=roots_hbm.at[i, pl.ds(pl.multiple_of(peer * rows_dev, 8), rows_dev)],
            dst_ref=slices[i].at[me],
            send_sem=c_s.at[i, t],
            recv_sem=c_r.at[i, me],
            device_id=(peer, z),
            device_id_type=MESH,
        )

    load_g.wait()

    def rows(k):
        return pl.ds(k * step, step)

    def piece(d, k):
        return g.at[rows(k), pl.ds(pl.multiple_of(d * cols, 128), cols)]

    def right(k, dist, first):
        return pltpu.make_async_remote_copy(
            src_ref=piece(z + dist, k) if first else rout.at[k, dist - 1],
            dst_ref=rin.at[k, dist - 1],
            send_sem=rs.at[k, dist - 1],
            recv_sem=rr.at[k, dist - 1],
            device_id=(me, z + 1),
            device_id_type=MESH,
        )

    def left(k, dist, first):
        return pltpu.make_async_remote_copy(
            src_ref=piece(z - dist, k) if first else lout.at[k, dist - 1],
            dst_ref=lin.at[k, dist - 1],
            send_sem=ls.at[k, dist - 1],
            recv_sem=lr.at[k, dist - 1],
            device_id=(me, z - 1),
            device_id_type=MESH,
        )

    def arrived(buffer, sem, k, slot):
        pltpu.make_async_copy(buffer.at[k, slot], buffer.at[k, slot], sem.at[k, slot]).wait()

    @pl.when(z == 0)
    def _():
        for dist in range(reps - 1, 0, -1):
            for k in range(chunks):
                right(k, dist, True).start()

    @pl.when(z == reps - 1)
    def _():
        for dist in range(reps - 1, 0, -1):
            for k in range(chunks):
                left(k, dist, True).start()

    for i in range(2):
        for t in range(shards - 1, 0, -1):
            cut(i, t).start()

    def to_home(j, src, dst, send, recv):
        return pltpu.make_async_remote_copy(
            src_ref=src,
            dst_ref=dst,
            send_sem=send,
            recv_sem=recv,
            device_id=(mix(mine, j, blocks) * per, z),
            device_id_type=MESH,
        )

    def lend(i, j):
        return to_home(j, chosen.at[i, j], roots.at[i, me], d_s.at[i, j], d_r.at[i, me])

    def spread(k, j):
        b = mix(mine, j, blocks)
        return to_home(j, full.at[k, b], gbuf.at[me, rows(k)], a_s.at[k, j], a_r.at[k, me])

    def landed(ref, sem):
        pltpu.make_async_copy(ref, ref, sem).wait()

    def pass_on(i):
        for t in range(shards - 1, 0, -1):
            peer = unmix(me, t, shards)
            landed(slices[i].at[peer], c_r.at[i, peer])
        for j in range(blocks - 1, 0, -1):
            chosen[i, j] = slices[i][owner[0, mix(mine, j, blocks)]]
            lend(i, j).start()

        @pl.when(is_home)
        def _():
            roots[i, me] = slices[i][owner[0, mine]]

        @pl.when(not_home)
        def _():
            chosen[i, 0] = slices[i][owner[0, mine]]
            lend(i, 0).start()

    for copy in keep:
        copy.wait()
    for dist in range(reps - 2, 0, -1):
        if dist == 1:
            pass_on(0)
        for k in range(chunks):

            @pl.when(jnp.logical_and(z > 0, z + dist <= reps - 1))
            def _():
                arrived(rin, rr, k, dist)
                mine = piece(z + dist, k)[...].astype(F32)
                rout[k, dist - 1] = (rin[k, dist].astype(F32) + mine).astype(BF16)
                right(k, dist, False).start()

            @pl.when(jnp.logical_and(z < reps - 1, z - dist >= 0))
            def _():
                arrived(lin, lr, k, dist)
                mine = piece(z - dist, k)[...].astype(F32)
                lout[k, dist - 1] = (lin[k, dist].astype(F32) + mine).astype(BF16)
                left(k, dist, False).start()

    for i in range(1 if reps > 2 else 0, 2):
        pass_on(i)

    for k in range(chunks):
        acc[...] = piece(z, k)[...].astype(F32)

        @pl.when(z > 0)
        def _():
            arrived(rin, rr, k, 0)
            acc[...] += rin[k, 0].astype(F32)

        @pl.when(z < reps - 1)
        def _():
            arrived(lin, lr, k, 0)
            acc[...] += lin[k, 0].astype(F32)

        for b in range(blocks):
            full[k, b] = acc[:, b * width : (b + 1) * width].astype(BF16)
        for j in range(blocks - 1, 0, -1):
            spread(k, j).start()

        @pl.when(is_home)
        def _():
            gbuf[me, k * step : (k + 1) * step] = full[k, mine]

        @pl.when(not_home)
        def _():
            spread(k, 0).start()

    def give(peer):
        return pltpu.make_async_remote_copy(
            src_ref=ubuf.at[peer],
            dst_ref=place(mine),
            send_sem=b_s.at[peer],
            recv_sem=b_r.at[mine],
            device_id=(peer, z),
            device_id_type=MESH,
        )

    def give_scale(t):
        peer = mix(me, t, shards)
        return pltpu.make_async_remote_copy(
            src_ref=gscale,
            dst_ref=scale_place(mine),
            send_sem=e_s.at[t],
            recv_sem=e_r.at[mine],
            device_id=(peer, z),
            device_id_type=MESH,
        )

    def scale_place(b):
        return scales.at[:, pl.ds(pl.multiple_of(b * width, 128), width)]

    def send_rows(s):
        @pl.when(me != s)
        def _():
            give(s).start()

    def place(b):
        return out.at[:, pl.ds(pl.multiple_of(b * width, 128), width)]

    def landed_roots():
        for i in range(2):
            for t in range(shards - 1, 0, -1):
                peer = unmix(me, t, shards)
                landed(roots.at[i, peer], d_r.at[i, peer])

    put_scale = pltpu.make_async_copy(gscale, scale_place(mine), load_sem.at[4])
    put = pltpu.make_async_copy(ubuf.at[me], place(mine), load_sem.at[3])

    @pl.when(is_home)
    def _():
        for k in range(chunks):
            for t in range(shards - 1, 0, -1):
                peer = unmix(me, t, shards)
                landed(gbuf.at[peer, rows(k)], a_r.at[k, peer])
        precondition(shards, rows_dev, refresh, mine, gbuf, roots, ubuf, landed_roots, gscale, send_rows)
        for t in range(shards - 1, 0, -1):
            give_scale(t).start()
        put.start()
        put_scale.start()

    for j in range(blocks - 1, 0, -1):
        b = unmix(mine, j, blocks)
        landed(place(b), b_r.at[b])
        landed(scale_place(b), e_r.at[b])

    @pl.when(not_home)
    def _():
        landed(place(mine), b_r.at[mine])
        landed(scale_place(mine), e_r.at[mine])
        for i in range(2):
            lend(i, 0).wait_send()
        for k in range(chunks):
            spread(k, 0).wait_send()

    @pl.when(is_home)
    def _():
        put.wait()
        put_scale.wait()
        for t in range(1, shards):
            give(mix(me, t, shards)).wait_send()
            give_scale(t).wait_send()

    for t in range(1, shards):
        for i in range(2):
            cut(i, t).wait_send()
    for j in range(1, blocks):
        for i in range(2):
            lend(i, j).wait_send()
        for k in range(chunks):
            spread(k, j).wait_send()
    for k in range(chunks):
        for dist in range(1, reps):

            @pl.when(z + dist <= reps - 1)
            def _():
                right(k, dist, False).wait_send()

            @pl.when(z - dist >= 0)
            def _():
                left(k, dist, False).wait_send()


def local(grad_parts, owner_plan, refresh, roots):
    shards = lax.axis_size("shard")
    reps = lax.axis_size("rep")
    _, rows_dev, all_cols = grad_parts.shape
    width = roots.shape[-1]
    blocks = owner_plan.shape[-1]
    cols = blocks * width
    chunks = max(1, min(2, rows_dev // 16))
    step = rows_dev // chunks
    hops = max(1, reps - 1)
    dma = pltpu.SemaphoreType.DMA
    anywhere = pl.BlockSpec(memory_space=pl.ANY)
    scalars = pl.BlockSpec(memory_space=pltpu.SMEM)
    moved, scales = pl.pallas_call(
        functools.partial(kernel, reps, shards, chunks),
        out_shape=(pltpu.VMEM((rows_dev, cols), BF16), pltpu.VMEM((8, cols), F32)),
        in_specs=[scalars, scalars, anywhere, anywhere],
        out_specs=(pl.BlockSpec(memory_space=pltpu.VMEM), pl.BlockSpec(memory_space=pltpu.VMEM)),
        scratch_shapes=[
            pltpu.VMEM((rows_dev, all_cols), BF16),
            pltpu.VMEM((chunks, hops, step, cols), BF16),
            pltpu.VMEM((chunks, hops, step, cols), BF16),
            pltpu.VMEM((chunks, hops, step, cols), BF16),
            pltpu.VMEM((chunks, hops, step, cols), BF16),
            pltpu.VMEM((step, cols), F32),
            pltpu.VMEM((chunks, blocks, step, width), BF16),
            pltpu.VMEM((shards, rows_dev, width), BF16),
            pltpu.VMEM((shards, rows_dev, width), BF16),
            pltpu.VMEM((shards, rows_dev, width), BF16),
            pltpu.VMEM((shards, rows_dev, width), BF16),
            pltpu.VMEM((2, blocks, rows_dev, width), BF16),
            pltpu.VMEM((2, shards, rows_dev, width), BF16),
            pltpu.VMEM((8, width), F32),
            dma((5,)),
            dma((chunks, hops)),
            dma((chunks, hops)),
            dma((chunks, hops)),
            dma((chunks, hops)),
            dma((chunks, blocks)),
            dma((chunks, shards)),
            dma((shards,)),
            dma((blocks,)),
            dma((shards,)),
            dma((blocks,)),
            dma((2, shards)),
            dma((2, shards)),
            dma((2, blocks)),
            dma((2, shards)),
        ],
        compiler_params=pltpu.CompilerParams(
            collective_id=0, has_side_effects=True, vmem_limit_bytes=60 * 1024 * 1024
        ),
    )(owner_plan, refresh, grad_parts[0], roots[0, 0])
    return (moved.astype(F32) * scales[:1]).astype(BF16)


def solution(mesh):
    placed = (
        P("rep", "shard", None),
        P("rep", None),
        P("rep", None),
        P("rep", "shard", None, None, None),
    )
    return jax.shard_map(
        local, mesh=mesh, in_specs=placed, out_specs=P("shard", "rep"), check_vma=False
    )
```
